256 devices in a mesh: blk: 64 (over z, x, y_hi), aux: 4 (over y_lo, core).
Axes of the slice: x: 4, y: 4 (y_hi: 2, y_lo: 2; y = y_hi * 2 + y_lo), z: 8, core: 2. Of those that a mesh axis runs over, the one named last changes fastest.
Arguments:
- coeffs: bfloat16 [16384, 512], P('blk'), may hold values from -6 to 6
- fitting: bfloat16 [16384, 256, 256], P('blk', 'aux'), may hold values from -0.375 to 0.375
- screen: int32 [256, 4], P('blk'), may hold values from 0 to 255, as said below
- counts: int32 [256], P('blk'), may hold values from 1 to 4, as said below
- tile_order: int32 [64, 16], P('blk'), may hold values from 0 to 15, each once within a row
Outputs:
- fock_tiles: float32 [1024, 4096], P(('blk', 'aux'))
The draws below stay inside these ranges and needn't reach their ends.
Inputs may be any that keep to these rules, and one draw needn't show every extreme that they name: `screen`: each partner block lies on the same index of blk as its basis block or on one of the two indices before or after it, counted around the axis. `counts`: some block uses all 4 slots and some block only one.
All inputs are finite; a program needn't handle non-finite values.
Results may differ from the reference program's by a relative error of at most 0.0003.
Values may be sent and summed in bfloat16 or wider, within the bound.
A program may use at most 128 MiB of HBM per device.

```python
import jax
import jax.numpy as jnp
from jax import lax

BS = 64
BLK_DEV = 4
SLOTS = 4
OCC = 512
NBLK = 256
NBAS = 16384
NAUX = 256
TILES = 16
N_BLK = 64


def draw_screen(key, part):
    first, second = jax.random.split(jax.random.fold_in(key, 11))
    offsets = jax.random.randint(first, (NBLK, SLOTS), -2, 3)
    inner = jax.random.randint(second, (NBLK, SLOTS), 0, BLK_DEV)
    groups = NBLK // BLK_DEV
    home = jnp.arange(NBLK, dtype=jnp.int32) // BLK_DEV
    return ((home[:, None] + offsets + groups) % groups * BLK_DEV + inner).astype(jnp.int32)


def draw_counts(key, part):
    values = jax.random.randint(jax.random.fold_in(key, 23), (NBLK,), 1, SLOTS + 1)
    values = values.at[0].set(SLOTS)
    values = values.at[1].set(1)
    return values.astype(jnp.int32)


def shard_levels(key, extent, pieces, smallest, largest):
    def one(axis_at, blocks):
        heights = jax.random.uniform(jax.random.fold_in(jax.random.fold_in(key, 6), axis_at), (blocks,), jnp.float32, smallest / len(pieces), largest / len(pieces))
        return jnp.repeat(jnp.exp(heights), extent[axis_at] // blocks).reshape((-1,) + (1,) * (len(extent) - axis_at - 1))

    gain = one(*pieces[0])
    for cut in pieces[1:]:
        gain = gain * one(*cut)
    return gain


def noise(rng, shape, width, most, cuts=(), kind=jnp.bfloat16):
    loudness = shard_levels(rng, shape, cuts, -0.22, 0.18) if cuts else 1.0
    values = jax.random.normal(rng, shape, jnp.float32) * width * loudness
    return jnp.minimum(jnp.maximum(values, -most), most).astype(kind)


def setup_inputs(seed: int = 0) -> dict:
    keys = jax.random.split(jax.random.key(seed), 6)
    return {
        "coeffs": noise(keys[0], (NBAS, OCC), 1.0, 6.0, ((0, 64),)),
        "fitting": noise(keys[1], (NBAS, NAUX, SLOTS * BS), (SLOTS * BS) ** -0.5, 0.375, ((0, 64), (1, 4))),
        "screen": draw_screen(jax.random.fold_in(keys[5], 71), 0),
        "counts": draw_counts(jax.random.fold_in(keys[5], 71), 0),
        "tile_order": jax.vmap(lambda own: jax.random.permutation(own, TILES))(jax.random.split(keys[4], N_BLK)).reshape((N_BLK, TILES)).astype(jnp.int32),
    }


def one_group(inputs, coeff_blocks):
    fitting_group, screen_group, count_group, order_group = inputs
    slot_index = jnp.arange(SLOTS, dtype=jnp.int32)
    keep_slot = (slot_index[None, :] < count_group[:, None]).astype(jnp.float32)
    picked = coeff_blocks[screen_group].astype(jnp.float32) * keep_slot[:, :, None, None]
    picked = picked.reshape(BLK_DEV, SLOTS * BS, OCC)
    fit_blocks = fitting_group.reshape(BLK_DEV, BS, NAUX, SLOTS * BS).astype(jnp.float32)
    half = jnp.einsum('mupl,mli->mupi', fit_blocks, picked).astype(jnp.bfloat16)
    flat = half.reshape(BS * BLK_DEV, NAUX * OCC)
    gram = jnp.dot(flat, flat.T, preferred_element_type=jnp.float32) / jnp.sqrt(jnp.float32(NAUX * OCC))
    tiles = gram.reshape(BLK_DEV, BS, BLK_DEV, BS).transpose(0, 2, 1, 3).reshape(TILES, BS * BS)
    return tiles[order_group]

def reference(coeffs, fitting, screen, counts, tile_order):
    coeff_blocks = coeffs.reshape(NBLK, BS, OCC)
    groups = (fitting.reshape(N_BLK, BS * BLK_DEV, NAUX, SLOTS * BS), screen.reshape(N_BLK, BLK_DEV, SLOTS), counts.reshape(N_BLK, BLK_DEV), tile_order)
    result = lax.map(lambda item: one_group(item, coeff_blocks), groups)
    return result.reshape(N_BLK * TILES, BS * BS)
```

```python
import functools

import jax
import jax.numpy as jnp
from jax import lax
from jax.experimental import pallas as pl
from jax.experimental.pallas import tpu as pltpu
from jax.sharding import PartitionSpec as P

MESH = pl.DeviceIdType.MESH
BF16, F32 = jnp.bfloat16, jnp.float32
CHUNK = 256
STEPS = (-2, -1, 1, 2)


def kernel(
    n_blk, scale, screen, counts, order, coeffs, fitting, out,
    raw, turned, window_a, window_b, picked, half, gram, tiles, ready, first_in, middle, second_in, total,
    load_sem, own_sem, send_sem, near_sem, pass_sem, share_sem, red_send, red_recv,
):
    position = lax.axis_index("blk")
    aux = lax.axis_index("aux")
    y_lo, core = aux // 2, lax.rem(aux, 2)
    blocks, slots = screen.shape
    _, width, orbitals = coeffs.shape
    rows = blocks * width
    aux_here = turned.shape[0]
    chunks = orbitals // CHUNK
    windows = [window_a, window_b]
    share = blocks // 2
    strip = raw.shape[0] // load_sem.shape[0]

    def device(blk, a):
        return {"blk": blk, "aux": a}

    sibling = device(position, y_lo * 2 + 1 - core)
    across = device(position, (1 - y_lo) * 2 + core)
    partners = {}
    for step in STEPS:
        to_aux = aux if step % 2 == 0 else (1 - y_lo) * 2 + core
        partners[step] = device(lax.rem(position + step + n_blk, n_blk), to_aux)

    def load(c):
        at = pl.ds(pl.multiple_of(c * strip, strip), strip)
        return pltpu.make_async_copy(fitting.at[at], raw.at[at], load_sem.at[c])

    for c in range(load_sem.shape[0]):
        load(c).start()
    own = [
        pltpu.make_async_copy(
            coeffs.at[:, :, ch * CHUNK : (ch + 1) * CHUNK],
            windows[ch].at[2 * blocks : 3 * blocks],
            own_sem.at[ch],
        )
        for ch in range(chunks)
    ]
    for copy in own:
        copy.start()

    barrier = pltpu.get_barrier_semaphore()
    everyone = [*partners.values(), sibling, across]
    for who in everyone:
        pl.semaphore_signal(barrier, inc=1, device_id=who, device_id_type=MESH)
    pl.semaphore_wait(barrier, len(everyone))

    sent, passed = {}, {}
    for ch in range(chunks):
        for n, step in enumerate(STEPS):
            lands = windows[ch].at[pl.ds((2 - step) * blocks + core * share, share)]
            sent[ch, n] = pltpu.make_async_remote_copy(
                src_ref=coeffs.at[pl.ds(core * share, share), :, ch * CHUNK : (ch + 1) * CHUNK],
                dst_ref=lands,
                send_sem=send_sem.at[ch, n],
                recv_sem=near_sem.at[ch, n],
                device_id=partners[step],
                device_id_type=MESH,
            )
            sent[ch, n].start()
            passed[ch, n] = pltpu.make_async_remote_copy(
                src_ref=lands,
                dst_ref=lands,
                send_sem=pass_sem.at[ch, n],
                recv_sem=share_sem.at[ch, n],
                device_id=sibling,
                device_id_type=MESH,
            )

    @pl.loop(0, load_sem.shape[0])
    def _(c):
        load(c).wait()
        at = pl.ds(pl.multiple_of(c * strip, strip), strip)
        for p in range(0, aux_here, 16):
            turned[p : p + 16, at, :] = jnp.swapaxes(raw[at, p : p + 16, :], 0, 1)

    def forward(ch):
        for n in range(len(STEPS)):
            sent[ch, n].wait_recv()
            passed[ch, n].start()

    def pick(ch):
        own[ch].wait()
        for n in range(len(STEPS)):
            passed[ch, n].wait_recv()
        for m in range(blocks):
            for s in range(slots):
                block = screen[m, s]
                away = lax.rem(block // blocks - position + 2 + n_blk, n_blk)
                away = jnp.minimum(away, len(STEPS))
                piece = windows[ch][away * blocks + lax.rem(block, blocks)]
                kept = jnp.where(s < counts[m], piece, jnp.zeros_like(piece))
                picked[ch, m, s * width : (s + 1) * width, :] = kept

    def contract(ch):
        for m in range(blocks):
            at = slice(m * width, (m + 1) * width)
            left = turned[:, at, :].reshape(aux_here * width, slots * width)
            got = jnp.dot(left, picked[ch, m], preferred_element_type=F32).astype(BF16)
            half[ch, :, at, :] = got.reshape(aux_here, width, CHUNK)

    def square(ch):
        flat = jnp.concatenate([half[ch, p] for p in range(aux_here)], axis=1)
        got = lax.dot_general(flat, flat, (((1,), (1,)), ((), ())), preferred_element_type=F32)
        for q in range(rows // 128):
            part = got[:, 128 * q : 128 * q + 128]
            gram[q] = part if ch == 0 else gram[q] + part

    forward(0)
    pick(0)
    for ch in range(chunks):
        contract(ch)
        if ch + 1 < chunks:
            forward(ch + 1)
        square(ch)
        if ch + 1 < chunks:
            pick(ch + 1)

    low = lax.broadcasted_iota(jnp.int32, (width // 2, 128), 1) < width
    for j in range(blocks):
        for q in range(rows // 128):
            even = gram[q, pl.ds(j * width, width // 2, stride=2), :]
            odd = gram[q, pl.ds(j * width + 1, width // 2, stride=2), :]
            tiles[j * blocks + 2 * q] = jnp.where(low, even, pltpu.roll(odd, 64, 1))
            tiles[j * blocks + 2 * q + 1] = jnp.where(low, pltpu.roll(even, 64, 1), odd)
    for o in range(tiles.shape[0]):
        ready[(o // 4) % 2, o // 8, o % 4] = tiles[order[0, o]]

    def reduce_copy(src, dst, n, who):
        return pltpu.make_async_remote_copy(
            src_ref=src, dst_ref=dst, send_sem=red_send.at[n], recv_sem=red_recv.at[n],
            device_id=who, device_id_type=MESH,
        )

    far, home = 1 - y_lo, y_lo
    away = reduce_copy(ready.at[1 - core, far], first_in.at[0], 0, sibling)
    here = reduce_copy(ready.at[1 - core, home], first_in.at[1], 1, sibling)
    cross = reduce_copy(middle, second_in, 2, across)
    away.start()
    here.start()
    away.wait_recv()
    middle[...] = ready[core, far] + first_in[0]
    cross.start()
    here.wait_recv()
    total[...] = ready[core, home] + first_in[1]
    cross.wait_recv()
    total[...] = (total[...] + second_in[...]) * scale
    for s in range(total.shape[1]):
        out[:, 128 * s : 128 * s + 128] = total[:, s, :]
    for copy in [*sent.values(), *passed.values(), away, here, cross]:
        copy.wait_send()


def per_device(coeffs, fitting, screen, counts, tile_order):
    rows, orbitals = coeffs.shape
    _, aux_here, inner = fitting.shape
    blocks, _ = screen.shape
    chunks = orbitals // CHUNK
    near = len(STEPS)
    side = rows // blocks
    n_tiles = tile_order.shape[1]
    kept = n_tiles // lax.axis_size("aux")
    tile = (side * side // 128, 128)
    scale = 1.0 / (aux_here * lax.axis_size("aux") * orbitals) ** 0.5
    smem = pl.BlockSpec(memory_space=pltpu.SMEM)
    hbm = pl.BlockSpec(memory_space=pl.ANY)
    return pl.pallas_call(
        functools.partial(kernel, lax.axis_size("blk"), scale),
        out_shape=jax.ShapeDtypeStruct((kept, side * side), F32),
        in_specs=[smem, smem, smem, hbm, hbm],
        out_specs=pl.BlockSpec(memory_space=pltpu.VMEM),
        scratch_shapes=[
            pltpu.VMEM((rows, aux_here, inner), BF16),
            pltpu.VMEM((aux_here, rows, inner), BF16),
            pltpu.VMEM(((near + 1) * blocks, side, CHUNK), BF16),
            pltpu.VMEM(((near + 1) * blocks, side, CHUNK), BF16),
            pltpu.VMEM((chunks, blocks, inner, CHUNK), BF16),
            pltpu.VMEM((chunks, aux_here, rows, CHUNK), BF16),
            pltpu.VMEM((rows // 128, rows, 128), F32),
            pltpu.VMEM((n_tiles, *tile), F32),
            pltpu.VMEM((2, 2, kept, *tile), F32),
            pltpu.VMEM((2, kept, *tile), F32),
            pltpu.VMEM((kept, *tile), F32),
            pltpu.VMEM((kept, *tile), F32),
            pltpu.VMEM((kept, *tile), F32),
            pltpu.SemaphoreType.DMA((16,)),
            pltpu.SemaphoreType.DMA((chunks,)),
            pltpu.SemaphoreType.DMA((chunks, near)),
            pltpu.SemaphoreType.DMA((chunks, near)),
            pltpu.SemaphoreType.DMA((chunks, near)),
            pltpu.SemaphoreType.DMA((chunks, near)),
            pltpu.SemaphoreType.DMA((3,)),
            pltpu.SemaphoreType.DMA((3,)),
        ],
        compiler_params=pltpu.CompilerParams(
            collective_id=0, has_side_effects=True, vmem_limit_bytes=60 << 20
        ),
    )(screen, counts, tile_order, coeffs.reshape(blocks, side, orbitals), fitting)


def solution(mesh):
    placed = (P("blk", None), P("blk", "aux", None), P("blk", None), P("blk"), P("blk", None))
    with jax.sharding.use_abstract_mesh(mesh.abstract_mesh):
        return jax.shard_map(
            per_device, mesh=mesh, in_specs=placed, out_specs=P(("blk", "aux"), None), check_vma=False
        )
```

```python
import functools

import jax
import jax.numpy as jnp
from jax import lax
from jax.experimental import pallas as pl
from jax.experimental.pallas import tpu as pltpu
from jax.sharding import PartitionSpec as P

MESH = pl.DeviceIdType.MESH
BF16, F32 = jnp.bfloat16, jnp.float32
CHUNK = 256
STEPS = (-2, -1, 1, 2)


def kernel(
    n_blk, scale, screen, counts, order, coeffs, fitting, out,
    raw, turned, window_a, window_b, picked, half, gram, tiles, ready, first_in, middle, second_in, total,
    load_sem, own_sem, send_sem, near_sem, pass_sem, share_sem, red_send, red_recv,
):
    position = lax.axis_index("blk")
    aux = lax.axis_index("aux")
    y_lo, core = aux // 2, lax.rem(aux, 2)
    blocks, slots = screen.shape
    _, width, orbitals = coeffs.shape
    rows = blocks * width
    aux_here = turned.shape[0]
    chunks = orbitals // CHUNK
    windows = [window_a, window_b]
    share = blocks // 2
    strip = raw.shape[0] // load_sem.shape[0]

    def device(blk, a):
        return {"blk": blk, "aux": a}

    sibling = device(position, y_lo * 2 + 1 - core)
    across = device(position, (1 - y_lo) * 2 + core)
    partners = {}
    for step in STEPS:
        to_aux = aux if step % 2 == 0 else (1 - y_lo) * 2 + core
        partners[step] = device(lax.rem(position + step + n_blk, n_blk), to_aux)

    def load(c):
        at = pl.ds(pl.multiple_of(c * strip, strip), strip)
        return pltpu.make_async_copy(fitting.at[at], raw.at[at], load_sem.at[c])

    for c in range(load_sem.shape[0]):
        load(c).start()
    own = [
        pltpu.make_async_copy(
            coeffs.at[:, :, ch * CHUNK : (ch + 1) * CHUNK],
            windows[ch].at[2 * blocks : 3 * blocks],
            own_sem.at[ch],
        )
        for ch in range(chunks)
    ]
    for copy in own:
        copy.start()

    barrier = pltpu.get_barrier_semaphore()
    everyone = [*partners.values(), sibling, across]
    for who in everyone:
        pl.semaphore_signal(barrier, inc=1, device_id=who, device_id_type=MESH)
    pl.semaphore_wait(barrier, len(everyone))

    sent, passed = {}, {}
    for ch in range(chunks):
        for n, step in enumerate(STEPS):
            lands = windows[ch].at[pl.ds((2 - step) * blocks + core * share, share)]
            sent[ch, n] = pltpu.make_async_remote_copy(
                src_ref=coeffs.at[pl.ds(core * share, share), :, ch * CHUNK : (ch + 1) * CHUNK],
                dst_ref=lands,
                send_sem=send_sem.at[ch, n],
                recv_sem=near_sem.at[ch, n],
                device_id=partners[step],
                device_id_type=MESH,
            )
            sent[ch, n].start()
            passed[ch, n] = pltpu.make_async_remote_copy(
                src_ref=lands,
                dst_ref=lands,
                send_sem=pass_sem.at[ch, n],
                recv_sem=share_sem.at[ch, n],
                device_id=sibling,
                device_id_type=MESH,
            )

    @pl.loop(0, load_sem.shape[0])
    def _(c):
        load(c).wait()
        at = pl.ds(pl.multiple_of(c * strip, strip), strip)
        for p in range(0, aux_here, 16):
            turned[p : p + 16, at, :] = jnp.swapaxes(raw[at, p : p + 16, :], 0, 1)

    def forward(ch):
        for n in range(len(STEPS)):
            sent[ch, n].wait_recv()
            passed[ch, n].start()

    def pick(ch):
        own[ch].wait()
        for n in range(len(STEPS)):
            passed[ch, n].wait_recv()
        for m in range(blocks):
            for s in range(slots):
                block = screen[m, s]
                away = lax.rem(block // blocks - position + 2 + n_blk, n_blk)
                away = jnp.minimum(away, len(STEPS))
                piece = windows[ch][away * blocks + lax.rem(block, blocks)]
                kept = jnp.where(s < counts[m], piece, jnp.zeros_like(piece))
                picked[ch, m, s * width : (s + 1) * width, :] = kept

    def contract(ch):
        @pl.loop(0, blocks // 2)
        def _(pair):
            for side in range(2):
                m = 2 * pair + side
                at = pl.ds(pl.multiple_of(m * width, width), width)
                left = turned[:, at, :].reshape(aux_here * width, slots * width)
                got = jnp.dot(left, picked[ch, m], preferred_element_type=F32).astype(BF16)
                half[ch, :, at, :] = got.reshape(aux_here, width, CHUNK)

    def square(ch):
        depth = aux_here // 2

        @pl.loop(0, 2)
        def _(part):
            flat = [half[ch, part * depth + p] for p in range(depth)]
            flat = jnp.concatenate(flat, axis=1)
            got = lax.dot_general(flat, flat, (((1,), (1,)), ((), ())), preferred_element_type=F32)
            for q in range(rows // 128):
                gram[q] += got[:, 128 * q : 128 * q + 128]

    gram[...] = jnp.zeros_like(gram)
    forward(0)
    pick(0)
    for ch in range(chunks):
        contract(ch)
        if ch + 1 < chunks:
            forward(ch + 1)
        square(ch)
        if ch + 1 < chunks:
            pick(ch + 1)

    low = lax.broadcasted_iota(jnp.int32, (width // 2, 128), 1) < width
    for j in range(blocks):
        for q in range(rows // 128):
            even = gram[q, pl.ds(j * width, width // 2, stride=2), :]
            odd = gram[q, pl.ds(j * width + 1, width // 2, stride=2), :]
            tiles[j * blocks + 2 * q] = jnp.where(low, even, pltpu.roll(odd, 64, 1))
            tiles[j * blocks + 2 * q + 1] = jnp.where(low, pltpu.roll(even, 64, 1), odd)
    for o in range(tiles.shape[0]):
        ready[(o // 4) % 2, o // 8, o % 4] = tiles[order[0, o]]

    def reduce_copy(src, dst, n, who):
        return pltpu.make_async_remote_copy(
            src_ref=src, dst_ref=dst, send_sem=red_send.at[n], recv_sem=red_recv.at[n],
            device_id=who, device_id_type=MESH,
        )

    far, home = 1 - y_lo, y_lo
    away = reduce_copy(ready.at[1 - core, far], first_in.at[0], 0, sibling)
    here = reduce_copy(ready.at[1 - core, home], first_in.at[1], 1, sibling)
    cross = reduce_copy(middle, second_in, 2, across)
    away.start()
    here.start()
    away.wait_recv()
    middle[...] = ready[core, far] + first_in[0]
    cross.start()
    here.wait_recv()
    total[...] = ready[core, home] + first_in[1]
    cross.wait_recv()
    total[...] = (total[...] + second_in[...]) * scale
    for s in range(total.shape[1]):
        out[:, 128 * s : 128 * s + 128] = total[:, s, :]
    for copy in [*sent.values(), *passed.values(), away, here, cross]:
        copy.wait_send()


def per_device(coeffs, fitting, screen, counts, tile_order):
    rows, orbitals = coeffs.shape
    _, aux_here, inner = fitting.shape
    blocks, _ = screen.shape
    chunks = orbitals // CHUNK
    near = len(STEPS)
    side = rows // blocks
    n_tiles = tile_order.shape[1]
    kept = n_tiles // lax.axis_size("aux")
    tile = (side * side // 128, 128)
    scale = 1.0 / (aux_here * lax.axis_size("aux") * orbitals) ** 0.5
    smem = pl.BlockSpec(memory_space=pltpu.SMEM)
    hbm = pl.BlockSpec(memory_space=pl.ANY)
    return pl.pallas_call(
        functools.partial(kernel, lax.axis_size("blk"), scale),
        out_shape=jax.ShapeDtypeStruct((kept, side * side), F32),
        in_specs=[smem, smem, smem, hbm, hbm],
        out_specs=pl.BlockSpec(memory_space=pltpu.VMEM),
        scratch_shapes=[
            pltpu.VMEM((rows, aux_here, inner), BF16),
            pltpu.VMEM((aux_here, rows, inner), BF16),
            pltpu.VMEM(((near + 1) * blocks, side, CHUNK), BF16),
            pltpu.VMEM(((near + 1) * blocks, side, CHUNK), BF16),
            pltpu.VMEM((chunks, blocks, inner, CHUNK), BF16),
            pltpu.VMEM((chunks, aux_here, rows, CHUNK), BF16),
            pltpu.VMEM((rows // 128, rows, 128), F32),
            pltpu.VMEM((n_tiles, *tile), F32),
            pltpu.VMEM((2, 2, kept, *tile), F32),
            pltpu.VMEM((2, kept, *tile), F32),
            pltpu.VMEM((kept, *tile), F32),
            pltpu.VMEM((kept, *tile), F32),
            pltpu.VMEM((kept, *tile), F32),
            pltpu.SemaphoreType.DMA((16,)),
            pltpu.SemaphoreType.DMA((chunks,)),
            pltpu.SemaphoreType.DMA((chunks, near)),
            pltpu.SemaphoreType.DMA((chunks, near)),
            pltpu.SemaphoreType.DMA((chunks, near)),
            pltpu.SemaphoreType.DMA((chunks, near)),
            pltpu.SemaphoreType.DMA((3,)),
            pltpu.SemaphoreType.DMA((3,)),
        ],
        compiler_params=pltpu.CompilerParams(
            collective_id=0, has_side_effects=True, vmem_limit_bytes=60 << 20
        ),
    )(screen, counts, tile_order, coeffs.reshape(blocks, side, orbitals), fitting)


def solution(mesh):
    placed = (P("blk", None), P("blk", "aux", None), P("blk", None), P("blk"), P("blk", None))
    with jax.sharding.use_abstract_mesh(mesh.abstract_mesh):
        return jax.shard_map(
            per_device, mesh=mesh, in_specs=placed, out_specs=P(("blk", "aux"), None), check_vma=False
        )
```

```python
import functools

import jax
import jax.numpy as jnp
from jax import lax
from jax.experimental import pallas as pl
from jax.experimental.pallas import tpu as pltpu
from jax.sharding import PartitionSpec as P

MESH = pl.DeviceIdType.MESH
BF16, F32 = jnp.bfloat16, jnp.float32
CHUNK = 256
STEPS = (-2, -1, 1, 2)


def kernel(
    n_blk, scale, screen, counts, order, coeffs, fitting, out,
    raw, turned, window_a, window_b, half, gram, tiles, ready, first_in, middle, second_in, total,
    load_sem, own_sem, send_sem, near_sem, pass_sem, share_sem, red_send, red_recv,
):
    position = lax.axis_index("blk")
    aux = lax.axis_index("aux")
    y_lo, core = aux // 2, lax.rem(aux, 2)
    blocks, slots = screen.shape
    _, width, orbitals = coeffs.shape
    rows = blocks * width
    aux_here = turned.shape[0]
    chunks = orbitals // CHUNK
    windows = [window_a, window_b]
    share = blocks // 2
    strip = raw.shape[0] // load_sem.shape[0]

    def device(blk, a):
        return {"blk": blk, "aux": a}

    sibling = device(position, y_lo * 2 + 1 - core)
    across = device(position, (1 - y_lo) * 2 + core)
    partners = {}
    for step in STEPS:
        to_aux = aux if step % 2 == 0 else (1 - y_lo) * 2 + core
        partners[step] = device(lax.rem(position + step + n_blk, n_blk), to_aux)

    barrier = pltpu.get_barrier_semaphore()
    everyone = [*partners.values(), sibling, across]
    for who in everyone:
        pl.semaphore_signal(barrier, inc=1, device_id=who, device_id_type=MESH)

    places = []
    for m in range(blocks):
        places.append([])
        for s in range(slots):
            block = screen[m, s]
            away = lax.rem(block // blocks - position + 2 + n_blk, n_blk)
            away = jnp.minimum(away, len(STEPS))
            places[m].append(away * blocks + lax.rem(block, blocks))

    def load(c):
        at = pl.ds(pl.multiple_of(c * strip, strip), strip)
        return pltpu.make_async_copy(fitting.at[at], raw.at[at], load_sem.at[c])

    pl.semaphore_wait(barrier, len(everyone))

    sent, passed = {}, {}
    for ch in range(chunks):
        for n, step in enumerate(STEPS):
            lands = windows[ch].at[pl.ds((2 - step) * blocks + core * share, share)]
            sent[ch, n] = pltpu.make_async_remote_copy(
                src_ref=coeffs.at[pl.ds(core * share, share), :, ch * CHUNK : (ch + 1) * CHUNK],
                dst_ref=lands,
                send_sem=send_sem.at[ch, n],
                recv_sem=near_sem.at[ch, n],
                device_id=partners[step],
                device_id_type=MESH,
            )
            if ch == 0:
                sent[ch, n].start()
            passed[ch, n] = pltpu.make_async_remote_copy(
                src_ref=lands,
                dst_ref=lands,
                send_sem=pass_sem.at[ch, n],
                recv_sem=share_sem.at[ch, n],
                device_id=sibling,
                device_id_type=MESH,
            )

    for c in range(load_sem.shape[0]):
        load(c).start()
    own = [
        pltpu.make_async_copy(
            coeffs.at[:, :, ch * CHUNK : (ch + 1) * CHUNK],
            windows[ch].at[2 * blocks : 3 * blocks],
            own_sem.at[ch],
        )
        for ch in range(chunks)
    ]
    for copy in own:
        copy.start()

    @pl.loop(0, load_sem.shape[0])
    def _(c):
        load(c).wait()
        at = pl.ds(pl.multiple_of(c * strip, strip), strip)
        for p in range(0, aux_here, 16):
            turned[p : p + 16, at, :] = jnp.swapaxes(raw[at, p : p + 16, :], 0, 1)

    def forward(ch):
        for n in range(len(STEPS)):
            sent[ch, n].wait_recv()
            passed[ch, n].start()

    def arrived(ch):
        own[ch].wait()
        for n in range(len(STEPS)):
            passed[ch, n].wait_recv()

    def picked(ch, m):
        pieces = []
        for s in range(slots):
            piece = windows[ch][places[m][s]]
            pieces.append(jnp.where(s < counts[m], piece, jnp.zeros_like(piece)))
        return jnp.concatenate(pieces, axis=0)

    once = 1 + position // n_blk

    def contract(ch):
        @pl.loop(0, once)
        def _(_):
            for m in range(blocks):
                at = slice(m * width, (m + 1) * width)
                left = turned[:, at, :].reshape(aux_here * width, slots * width)
                got = jnp.dot(left, picked(ch, m), preferred_element_type=F32).astype(BF16)
                half[ch, :, at, :] = got.reshape(aux_here, width, CHUNK)

    def square(ch, parts):
        depth = aux_here // 2

        @pl.loop(parts.start, parts.stop - 1 + once)
        def _(part):
            flat = [half[ch, part * depth + p] for p in range(depth)]
            flat = jnp.concatenate(flat, axis=1)
            got = lax.dot_general(flat, flat, (((1,), (1,)), ((), ())), preferred_element_type=F32)
            for q in range(rows // 128):
                gram[q] += got[:, 128 * q : 128 * q + 128]

    gram[...] = jnp.zeros_like(gram)
    for n in range(len(STEPS)):
        sent[0, n].wait_send()
        sent[1, n].start()
    forward(0)
    arrived(0)
    contract(0)
    square(0, range(0, 1))
    forward(1)
    square(0, range(1, 2))
    arrived(1)
    contract(1)
    square(1, range(0, 2))

    low = lax.broadcasted_iota(jnp.int32, (width // 2, 128), 1) < width
    for j in range(blocks):
        for q in range(rows // 128):
            even = gram[q, pl.ds(j * width, width // 2, stride=2), :]
            odd = gram[q, pl.ds(j * width + 1, width // 2, stride=2), :]
            tiles[j * blocks + 2 * q] = jnp.where(low, even, pltpu.roll(odd, 64, 1))
            tiles[j * blocks + 2 * q + 1] = jnp.where(low, pltpu.roll(even, 64, 1), odd)
    for o in range(tiles.shape[0]):
        ready[(o // 4) % 2, o // 8, o % 4] = tiles[order[0, o]]

    def reduce_copy(src, dst, n, who):
        return pltpu.make_async_remote_copy(
            src_ref=src, dst_ref=dst, send_sem=red_send.at[n], recv_sem=red_recv.at[n],
            device_id=who, device_id_type=MESH,
        )

    far, home = 1 - y_lo, y_lo
    away = reduce_copy(ready.at[1 - core, far], first_in.at[0], 0, sibling)
    here = reduce_copy(ready.at[1 - core, home], first_in.at[1], 1, sibling)
    cross = reduce_copy(middle, second_in, 2, across)
    away.start()
    here.start()
    away.wait_recv()
    middle[...] = ready[core, far] + first_in[0]
    cross.start()
    here.wait_recv()
    total[...] = ready[core, home] + first_in[1]
    cross.wait_recv()
    total[...] = (total[...] + second_in[...]) * scale
    for s in range(total.shape[1]):
        out[:, 128 * s : 128 * s + 128] = total[:, s, :]
    for copy in [*(sent[1, n] for n in range(len(STEPS))), *passed.values(), away, here, cross]:
        copy.wait_send()


def per_device(coeffs, fitting, screen, counts, tile_order):
    rows, orbitals = coeffs.shape
    _, aux_here, inner = fitting.shape
    blocks, _ = screen.shape
    chunks = orbitals // CHUNK
    near = len(STEPS)
    side = rows // blocks
    n_tiles = tile_order.shape[1]
    kept = n_tiles // lax.axis_size("aux")
    tile = (side * side // 128, 128)
    scale = 1.0 / (aux_here * lax.axis_size("aux") * orbitals) ** 0.5
    smem = pl.BlockSpec(memory_space=pltpu.SMEM)
    hbm = pl.BlockSpec(memory_space=pl.ANY)
    return pl.pallas_call(
        functools.partial(kernel, lax.axis_size("blk"), scale),
        out_shape=pltpu.VMEM((kept, side * side), F32),
        in_specs=[smem, smem, smem, hbm, hbm],
        out_specs=pl.BlockSpec(memory_space=pltpu.VMEM),
        scratch_shapes=[
            pltpu.VMEM((rows, aux_here, inner), BF16),
            pltpu.VMEM((aux_here, rows, inner), BF16),
            pltpu.VMEM(((near + 1) * blocks, side, CHUNK), BF16),
            pltpu.VMEM(((near + 1) * blocks, side, CHUNK), BF16),
            pltpu.VMEM((chunks, aux_here, rows, CHUNK), BF16),
            pltpu.VMEM((rows // 128, rows, 128), F32),
            pltpu.VMEM((n_tiles, *tile), F32),
            pltpu.VMEM((2, 2, kept, *tile), F32),
            pltpu.VMEM((2, kept, *tile), F32),
            pltpu.VMEM((kept, *tile), F32),
            pltpu.VMEM((kept, *tile), F32),
            pltpu.VMEM((kept, *tile), F32),
            pltpu.SemaphoreType.DMA((16,)),
            pltpu.SemaphoreType.DMA((chunks,)),
            pltpu.SemaphoreType.DMA((chunks, near)),
            pltpu.SemaphoreType.DMA((chunks, near)),
            pltpu.SemaphoreType.DMA((chunks, near)),
            pltpu.SemaphoreType.DMA((chunks, near)),
            pltpu.SemaphoreType.DMA((3,)),
            pltpu.SemaphoreType.DMA((3,)),
        ],
        compiler_params=pltpu.CompilerParams(
            collective_id=0, has_side_effects=True, vmem_limit_bytes=60 << 20
        ),
    )(screen, counts, tile_order, coeffs.reshape(blocks, side, orbitals), fitting)


def solution(mesh):
    placed = (P("blk", None), P("blk", "aux", None), P("blk", None), P("blk"), P("blk", None))
    with jax.sharding.use_abstract_mesh(mesh.abstract_mesh):
        return jax.shard_map(
            per_device, mesh=mesh, in_specs=placed, out_specs=P(("blk", "aux"), None), check_vma=False
        )
```

```python
import functools

import jax
import jax.numpy as jnp
from jax import lax
from jax.experimental import pallas as pl
from jax.experimental.pallas import tpu as pltpu
from jax.sharding import PartitionSpec as P

MESH = pl.DeviceIdType.MESH
BF16, F32 = jnp.bfloat16, jnp.float32
CHUNK = 256
STEPS = (-1, 1, -2, 2)


def kernel(
    n_blk, scale, screen, counts, order, coeffs, fitting, out,
    raw, turned, window_a, window_b, half, gram, tiles, ready, first_in, middle, second_in, total,
    load_sem, own_sem, send_sem, near_sem, pass_sem, share_sem, red_send, red_recv,
):
    position = lax.axis_index("blk")
    aux = lax.axis_index("aux")
    y_lo, core = aux // 2, lax.rem(aux, 2)
    blocks, slots = screen.shape
    _, width, orbitals = coeffs.shape
    rows = blocks * width
    aux_here = turned.shape[0]
    chunks = orbitals // CHUNK
    windows = [window_a, window_b]
    share = blocks // 2
    strip = raw.shape[0] // load_sem.shape[0]

    def device(blk, a):
        return {"blk": blk, "aux": a}

    sibling = device(position, y_lo * 2 + 1 - core)
    across = device(position, (1 - y_lo) * 2 + core)
    partners = {}
    for step in STEPS:
        to_aux = aux if step % 2 == 0 else (1 - y_lo) * 2 + core
        partners[step] = device(lax.rem(position + step + n_blk, n_blk), to_aux)

    barrier = pltpu.get_barrier_semaphore()
    everyone = [*partners.values(), sibling, across]
    for who in everyone:
        pl.semaphore_signal(barrier, inc=1, device_id=who, device_id_type=MESH)

    places = []
    for m in range(blocks):
        places.append([])
        for s in range(slots):
            block = screen[m, s]
            away = lax.rem(block // blocks - position + 2 + n_blk, n_blk)
            away = jnp.minimum(away, len(STEPS))
            places[m].append(away * blocks + lax.rem(block, blocks))

    def load(c):
        at = pl.ds(pl.multiple_of(c * strip, strip), strip)
        return pltpu.make_async_copy(fitting.at[at], raw.at[at], load_sem.at[c])

    own = [
        pltpu.make_async_copy(
            coeffs.at[:, :, ch * CHUNK : (ch + 1) * CHUNK],
            windows[ch].at[2 * blocks : 3 * blocks],
            own_sem.at[ch],
        )
        for ch in range(chunks)
    ]
    for copy in own:
        copy.start()
    pl.semaphore_wait(barrier, len(everyone))
    for copy in own:
        copy.wait()

    sent, passed = {}, {}
    for ch in range(chunks):
        for n, step in enumerate(STEPS):
            lands = windows[ch].at[pl.ds((2 - step) * blocks + core * share, share)]
            sent[ch, n] = pltpu.make_async_remote_copy(
                src_ref=windows[ch].at[pl.ds(2 * blocks + core * share, share)],
                dst_ref=lands,
                send_sem=send_sem.at[ch, n],
                recv_sem=near_sem.at[ch, n],
                device_id=partners[step],
                device_id_type=MESH,
            )
            if ch == 0:
                sent[ch, n].start()
            passed[ch, n] = pltpu.make_async_remote_copy(
                src_ref=lands,
                dst_ref=lands,
                send_sem=pass_sem.at[ch, n],
                recv_sem=share_sem.at[ch, n],
                device_id=sibling,
                device_id_type=MESH,
            )

    for c in range(load_sem.shape[0]):
        load(c).start()
    @pl.loop(0, load_sem.shape[0])
    def _(c):
        load(c).wait()
        at = pl.ds(pl.multiple_of(c * strip, strip), strip)
        for p in range(0, aux_here, 16):
            turned[p : p + 16, at, :] = jnp.swapaxes(raw[at, p : p + 16, :], 0, 1)

    def forward(ch):
        for n in (2, 3, 0, 1):
            sent[ch, n].wait_recv()
            passed[ch, n].start()

    def arrived(ch):
        for n in range(len(STEPS)):
            passed[ch, n].wait_recv()

    def picked(ch, m):
        pieces = []
        for s in range(slots):
            piece = windows[ch][places[m][s]]
            pieces.append(jnp.where(s < counts[m], piece, jnp.zeros_like(piece)))
        return jnp.concatenate(pieces, axis=0)

    once = 1 + position // n_blk

    def contract(ch):
        @pl.loop(0, once)
        def _(_):
            for m in range(blocks):
                at = slice(m * width, (m + 1) * width)
                left = turned[:, at, :].reshape(aux_here * width, slots * width)
                got = jnp.dot(left, picked(ch, m), preferred_element_type=F32).astype(BF16)
                half[ch, :, at, :] = got.reshape(aux_here, width, CHUNK)

    def square(ch, part, parts):
        depth = aux_here // parts

        @pl.loop(part, part + once)
        def _(at):
            flat = [half[ch, at * depth + p] for p in range(depth)]
            flat = jnp.concatenate(flat, axis=1)
            got = lax.dot_general(flat, flat, (((1,), (1,)), ((), ())), preferred_element_type=F32)
            for q in range(rows // 128):
                gram[q] += got[:, 128 * q : 128 * q + 128]

    gram[...] = jnp.zeros_like(gram)
    for n in range(len(STEPS)):
        sent[0, n].wait_send()
        sent[1, n].start()
    forward(0)
    arrived(0)
    contract(0)
    square(0, 0, 2)
    forward(1)
    square(0, 1, 2)
    arrived(1)
    contract(1)
    square(1, 0, 1)

    low = lax.broadcasted_iota(jnp.int32, (width // 2, 128), 1) < width
    for j in range(blocks):
        for q in range(rows // 128):
            even = gram[q, pl.ds(j * width, width // 2, stride=2), :]
            odd = gram[q, pl.ds(j * width + 1, width // 2, stride=2), :]
            tiles[j * blocks + 2 * q] = jnp.where(low, even, pltpu.roll(odd, 64, 1))
            tiles[j * blocks + 2 * q + 1] = jnp.where(low, pltpu.roll(even, 64, 1), odd)
    for o in range(tiles.shape[0]):
        ready[(o // 4) % 2, o // 8, o % 4] = tiles[order[0, o]]

    def reduce_copy(src, dst, n, who):
        return pltpu.make_async_remote_copy(
            src_ref=src, dst_ref=dst, send_sem=red_send.at[n], recv_sem=red_recv.at[n],
            device_id=who, device_id_type=MESH,
        )

    far, home = 1 - y_lo, y_lo
    away = reduce_copy(ready.at[1 - core, far], first_in.at[0], 0, sibling)
    here = reduce_copy(ready.at[1 - core, home], first_in.at[1], 1, sibling)
    cross = reduce_copy(middle, second_in, 2, across)
    away.start()
    here.start()
    away.wait_recv()
    middle[...] = ready[core, far] + first_in[0]
    cross.start()
    here.wait_recv()
    total[...] = ready[core, home] + first_in[1]
    cross.wait_recv()
    total[...] = (total[...] + second_in[...]) * scale
    for s in range(total.shape[1]):
        out[:, 128 * s : 128 * s + 128] = total[:, s, :]
    for copy in [*(sent[1, n] for n in range(len(STEPS))), *passed.values(), away, here, cross]:
        copy.wait_send()


def per_device(coeffs, fitting, screen, counts, tile_order):
    rows, orbitals = coeffs.shape
    _, aux_here, inner = fitting.shape
    blocks, _ = screen.shape
    chunks = orbitals // CHUNK
    near = len(STEPS)
    side = rows // blocks
    n_tiles = tile_order.shape[1]
    kept = n_tiles // lax.axis_size("aux")
    tile = (side * side // 128, 128)
    scale = 1.0 / (aux_here * lax.axis_size("aux") * orbitals) ** 0.5
    smem = pl.BlockSpec(memory_space=pltpu.SMEM)
    hbm = pl.BlockSpec(memory_space=pl.ANY)
    return pl.pallas_call(
        functools.partial(kernel, lax.axis_size("blk"), scale),
        out_shape=pltpu.VMEM((kept, side * side), F32),
        in_specs=[smem, smem, smem, hbm, hbm],
        out_specs=pl.BlockSpec(memory_space=pltpu.VMEM),
        scratch_shapes=[
            pltpu.VMEM((rows, aux_here, inner), BF16),
            pltpu.VMEM((aux_here, rows, inner), BF16),
            pltpu.VMEM(((near + 1) * blocks, side, CHUNK), BF16),
            pltpu.VMEM(((near + 1) * blocks, side, CHUNK), BF16),
            pltpu.VMEM((chunks, aux_here, rows, CHUNK), BF16),
            pltpu.VMEM((rows // 128, rows, 128), F32),
            pltpu.VMEM((n_tiles, *tile), F32),
            pltpu.VMEM((2, 2, kept, *tile), F32),
            pltpu.VMEM((2, kept, *tile), F32),
            pltpu.VMEM((kept, *tile), F32),
            pltpu.VMEM((kept, *tile), F32),
            pltpu.VMEM((kept, *tile), F32),
            pltpu.SemaphoreType.DMA((16,)),
            pltpu.SemaphoreType.DMA((chunks,)),
            pltpu.SemaphoreType.DMA((chunks, near)),
            pltpu.SemaphoreType.DMA((chunks, near)),
            pltpu.SemaphoreType.DMA((chunks, near)),
            pltpu.SemaphoreType.DMA((chunks, near)),
            pltpu.SemaphoreType.DMA((3,)),
            pltpu.SemaphoreType.DMA((3,)),
        ],
        compiler_params=pltpu.CompilerParams(
            collective_id=0, has_side_effects=True, vmem_limit_bytes=60 << 20
        ),
    )(screen, counts, tile_order, coeffs.reshape(blocks, side, orbitals), fitting)


def solution(mesh):
    placed = (P("blk", None), P("blk", "aux", None), P("blk", None), P("blk"), P("blk", None))
    with jax.sharding.use_abstract_mesh(mesh.abstract_mesh):
        return jax.shard_map(
            per_device, mesh=mesh, in_specs=placed, out_specs=P(("blk", "aux"), None), check_vma=False
        )
```

```python
import functools

import jax
import jax.numpy as jnp
from jax import lax
from jax.experimental import pallas as pl
from jax.experimental.pallas import tpu as pltpu
from jax.sharding import PartitionSpec as P

MESH = pl.DeviceIdType.MESH
BF16, F32 = jnp.bfloat16, jnp.float32
CHUNK = 256
STEPS = (-1, 1, -2, 2)


def kernel(
    n_blk, scale, screen, counts, order, coeffs, fitting, out,
    raw, turned, window_a, window_b, half, gram, tiles, ready, first_in, middle, second_in, total,
    load_sem, own_sem, send_sem, near_sem, pass_sem, share_sem, red_send, red_recv,
):
    position = lax.axis_index("blk")
    aux = lax.axis_index("aux")
    y_lo, core = aux // 2, lax.rem(aux, 2)
    blocks, slots = screen.shape
    _, width, orbitals = coeffs.shape
    rows = blocks * width
    aux_here = turned.shape[0]
    chunks = orbitals // CHUNK
    windows = [window_a, window_b]
    share = blocks // 2
    strip = raw.shape[0] // load_sem.shape[0]

    def device(blk, a):
        return {"blk": blk, "aux": a}

    sibling = device(position, y_lo * 2 + 1 - core)
    across = device(position, (1 - y_lo) * 2 + core)
    partners = {}
    for step in STEPS:
        to_aux = aux if step % 2 == 0 else (1 - y_lo) * 2 + core
        partners[step] = device(lax.rem(position + step + n_blk, n_blk), to_aux)

    barrier = pltpu.get_barrier_semaphore()
    everyone = [*partners.values(), sibling, across]
    for who in everyone:
        pl.semaphore_signal(barrier, inc=1, device_id=who, device_id_type=MESH)

    places = []
    for m in range(blocks):
        places.append([])
        for s in range(slots):
            block = screen[m, s]
            away = lax.rem(block // blocks - position + 2 + n_blk, n_blk)
            away = jnp.minimum(away, len(STEPS))
            places[m].append(away * blocks + lax.rem(block, blocks))

    def load(c):
        at = pl.ds(pl.multiple_of(c * strip, strip), strip)
        return pltpu.make_async_copy(fitting.at[at], raw.at[at], load_sem.at[c])

    own = [
        pltpu.make_async_copy(
            coeffs.at[:, :, ch * CHUNK : (ch + 1) * CHUNK],
            windows[ch].at[2 * blocks : 3 * blocks],
            own_sem.at[ch],
        )
        for ch in range(chunks)
    ]
    for copy in own:
        copy.start()
    pl.semaphore_wait(barrier, len(everyone))
    for copy in own:
        copy.wait()

    sent, passed = {}, {}
    for ch in range(chunks):
        for n, step in enumerate(STEPS):
            lands = windows[ch].at[pl.ds((2 - step) * blocks + core * share, share)]
            sent[ch, n] = pltpu.make_async_remote_copy(
                src_ref=windows[ch].at[pl.ds(2 * blocks + core * share, share)],
                dst_ref=lands,
                send_sem=send_sem.at[ch, n],
                recv_sem=near_sem.at[ch, n],
                device_id=partners[step],
                device_id_type=MESH,
            )
            if ch == 0:
                sent[ch, n].start()
            passed[ch, n] = pltpu.make_async_remote_copy(
                src_ref=lands,
                dst_ref=lands,
                send_sem=pass_sem.at[ch, n],
                recv_sem=share_sem.at[ch, n],
                device_id=sibling,
                device_id_type=MESH,
            )

    for c in range(load_sem.shape[0]):
        load(c).start()
    @pl.loop(0, load_sem.shape[0])
    def _(c):
        load(c).wait()
        at = pl.ds(pl.multiple_of(c * strip, strip), strip)
        for p in range(0, aux_here, 16):
            turned[p : p + 16, at, :] = jnp.swapaxes(raw[at, p : p + 16, :], 0, 1)

    def forward(ch):
        for n in (2, 3, 0, 1):
            sent[ch, n].wait_recv()
            passed[ch, n].start()

    def arrived(ch):
        for n in range(len(STEPS)):
            passed[ch, n].wait_recv()

    def picked(ch, m):
        pieces = []
        for s in range(slots):
            piece = windows[ch][places[m][s]]
            pieces.append(jnp.where(s < counts[m], piece, jnp.zeros_like(piece)))
        return jnp.concatenate(pieces, axis=0)

    once = 1 + position // n_blk

    def contract(ch):
        @pl.loop(0, once)
        def _(_):
            for m in range(blocks):
                at = slice(m * width, (m + 1) * width)
                left = turned[:, at, :].reshape(aux_here * width, slots * width)
                got = jnp.dot(left, picked(ch, m), preferred_element_type=F32).astype(BF16)
                half[ch, :, at, :] = got.reshape(aux_here, width, CHUNK)

    def square(ch, part, parts):
        depth = aux_here // parts

        @pl.loop(part, part + once)
        def _(at):
            flat = [half[ch, at * depth + p] for p in range(depth)]
            flat = jnp.concatenate(flat, axis=1)
            got = lax.dot_general(flat, flat, (((1,), (1,)), ((), ())), preferred_element_type=F32)
            for q in range(rows // 128):
                gram[q] += got[:, 128 * q : 128 * q + 128]

    gram[...] = jnp.zeros_like(gram)
    for n in range(len(STEPS)):
        sent[0, n].wait_send()
        sent[1, n].start()
    forward(0)
    arrived(0)
    contract(0)
    square(0, 0, 2)
    forward(1)
    square(0, 1, 2)
    arrived(1)
    contract(1)
    square(1, 0, 1)

    low = lax.broadcasted_iota(jnp.int32, (width // 2, 128), 1) < width
    for j in range(blocks):
        for q in range(rows // 128):
            even = gram[q, pl.ds(j * width, width // 2, stride=2), :]
            odd = gram[q, pl.ds(j * width + 1, width // 2, stride=2), :]
            tiles[j * blocks + 2 * q] = jnp.where(low, even, pltpu.roll(odd, 64, 1))
            tiles[j * blocks + 2 * q + 1] = jnp.where(low, pltpu.roll(even, 64, 1), odd)
    far, home = 1 - y_lo, y_lo
    kept = total.shape[0]

    def lay_out(to_core, to_side):
        for t in range(kept):
            o = (to_side * 2 + to_core) * kept + t
            ready[to_core, to_side, t] = tiles[order[0, o]]

    def reduce_copy(src, dst, n, who):
        return pltpu.make_async_remote_copy(
            src_ref=src, dst_ref=dst, send_sem=red_send.at[n], recv_sem=red_recv.at[n],
            device_id=who, device_id_type=MESH,
        )

    away = reduce_copy(ready.at[1 - core, far], first_in.at[0], 0, sibling)
    here = reduce_copy(ready.at[1 - core, home], first_in.at[1], 1, sibling)
    cross = [
        reduce_copy(middle.at[half_at], second_in.at[half_at], 2 + n, across)
        for n, half_at in enumerate((pl.ds(0, kept // 2), pl.ds(kept // 2, kept // 2)))
    ]
    lay_out(1 - core, far)
    away.start()
    lay_out(core, far)
    away.wait_recv()
    for n in range(2):
        at = slice(n * (kept // 2), (n + 1) * (kept // 2))
        middle[at] = ready[core, far, at] + first_in[0, at]
        cross[n].start()
    lay_out(1 - core, home)
    here.start()
    lay_out(core, home)
    here.wait_recv()
    total[...] = ready[core, home] + first_in[1]
    for copy in cross:
        copy.wait_recv()
    total[...] = (total[...] + second_in[...]) * scale
    for s in range(total.shape[1]):
        out[:, 128 * s : 128 * s + 128] = total[:, s, :]
    for copy in [*(sent[1, n] for n in range(len(STEPS))), *passed.values(), away, here, *cross]:
        copy.wait_send()


def per_device(coeffs, fitting, screen, counts, tile_order):
    rows, orbitals = coeffs.shape
    _, aux_here, inner = fitting.shape
    blocks, _ = screen.shape
    chunks = orbitals // CHUNK
    near = len(STEPS)
    side = rows // blocks
    n_tiles = tile_order.shape[1]
    kept = n_tiles // lax.axis_size("aux")
    tile = (side * side // 128, 128)
    scale = 1.0 / (aux_here * lax.axis_size("aux") * orbitals) ** 0.5
    smem = pl.BlockSpec(memory_space=pltpu.SMEM)
    hbm = pl.BlockSpec(memory_space=pl.ANY)
    return pl.pallas_call(
        functools.partial(kernel, lax.axis_size("blk"), scale),
        out_shape=pltpu.VMEM((kept, side * side), F32),
        in_specs=[smem, smem, smem, hbm, hbm],
        out_specs=pl.BlockSpec(memory_space=pltpu.VMEM),
        scratch_shapes=[
            pltpu.VMEM((rows, aux_here, inner), BF16),
            pltpu.VMEM((aux_here, rows, inner), BF16),
            pltpu.VMEM(((near + 1) * blocks, side, CHUNK), BF16),
            pltpu.VMEM(((near + 1) * blocks, side, CHUNK), BF16),
            pltpu.VMEM((chunks, aux_here, rows, CHUNK), BF16),
            pltpu.VMEM((rows // 128, rows, 128), F32),
            pltpu.VMEM((n_tiles, *tile), F32),
            pltpu.VMEM((2, 2, kept, *tile), F32),
            pltpu.VMEM((2, kept, *tile), F32),
            pltpu.VMEM((kept, *tile), F32),
            pltpu.VMEM((kept, *tile), F32),
            pltpu.VMEM((kept, *tile), F32),
            pltpu.SemaphoreType.DMA((16,)),
            pltpu.SemaphoreType.DMA((chunks,)),
            pltpu.SemaphoreType.DMA((chunks, near)),
            pltpu.SemaphoreType.DMA((chunks, near)),
            pltpu.SemaphoreType.DMA((chunks, near)),
            pltpu.SemaphoreType.DMA((chunks, near)),
            pltpu.SemaphoreType.DMA((4,)),
            pltpu.SemaphoreType.DMA((4,)),
        ],
        compiler_params=pltpu.CompilerParams(
            collective_id=0, has_side_effects=True, vmem_limit_bytes=60 << 20
        ),
    )(screen, counts, tile_order, coeffs.reshape(blocks, side, orbitals), fitting)


def solution(mesh):
    placed = (P("blk", None), P("blk", "aux", None), P("blk", None), P("blk"), P("blk", None))
    with jax.sharding.use_abstract_mesh(mesh.abstract_mesh):
        return jax.shard_map(
            per_device, mesh=mesh, in_specs=placed, out_specs=P(("blk", "aux"), None), check_vma=False
        )
```

```python
import functools

import jax
import jax.numpy as jnp
from jax import lax
from jax.experimental import pallas as pl
from jax.experimental.pallas import tpu as pltpu
from jax.sharding import PartitionSpec as P

MESH = pl.DeviceIdType.MESH
BF16, F32 = jnp.bfloat16, jnp.float32
CHUNK = 256
STEPS = (-1, 1, -2, 2)


def kernel(
    n_blk, scale, screen, counts, order, coeffs, fitting, out,
    raw, turned, window_a, window_b, half, gram, tiles, ready, first_in, middle, second_in, total,
    load_sem, own_sem, send_sem, near_sem, pass_sem, share_sem, red_send, red_recv,
):
    position = lax.axis_index("blk")
    aux = lax.axis_index("aux")
    y_lo, core = aux // 2, lax.rem(aux, 2)
    blocks, slots = screen.shape
    _, width, orbitals = coeffs.shape
    rows = blocks * width
    aux_here = turned.shape[0]
    chunks = orbitals // CHUNK
    windows = [window_a, window_b]
    share = blocks // 2
    strip = raw.shape[0] // load_sem.shape[0]

    def device(blk, a):
        return {"blk": blk, "aux": a}

    sibling = device(position, y_lo * 2 + 1 - core)
    across = device(position, (1 - y_lo) * 2 + core)
    partners = {}
    for step in STEPS:
        to_aux = aux if step % 2 == 0 else (1 - y_lo) * 2 + core
        partners[step] = device(lax.rem(position + step + n_blk, n_blk), to_aux)

    barrier = pltpu.get_barrier_semaphore()
    everyone = [*partners.values(), sibling, across]
    for who in everyone:
        pl.semaphore_signal(barrier, inc=1, device_id=who, device_id_type=MESH)

    places = []
    for m in range(blocks):
        places.append([])
        for s in range(slots):
            block = screen[m, s]
            away = lax.rem(block // blocks - position + 2 + n_blk, n_blk)
            away = jnp.minimum(away, len(STEPS))
            places[m].append(away * blocks + lax.rem(block, blocks))

    def load(c):
        at = pl.ds(pl.multiple_of(c * strip, strip), strip)
        return pltpu.make_async_copy(fitting.at[at], raw.at[at], load_sem.at[c])

    own = [
        pltpu.make_async_copy(
            coeffs.at[:, :, ch * CHUNK : (ch + 1) * CHUNK],
            windows[ch].at[2 * blocks : 3 * blocks],
            own_sem.at[ch],
        )
        for ch in range(chunks)
    ]
    for copy in own:
        copy.start()
    pl.semaphore_wait(barrier, len(everyone))
    for copy in own:
        copy.wait()

    sent, passed = {}, {}
    for ch in range(chunks):
        for n, step in enumerate(STEPS):
            lands = windows[ch].at[pl.ds((2 - step) * blocks + core * share, share)]
            sent[ch, n] = pltpu.make_async_remote_copy(
                src_ref=windows[ch].at[pl.ds(2 * blocks + core * share, share)],
                dst_ref=lands,
                send_sem=send_sem.at[ch, n],
                recv_sem=near_sem.at[ch, n],
                device_id=partners[step],
                device_id_type=MESH,
            )
            if ch == 0:
                sent[ch, n].start()
            passed[ch, n] = pltpu.make_async_remote_copy(
                src_ref=lands,
                dst_ref=lands,
                send_sem=pass_sem.at[ch, n],
                recv_sem=share_sem.at[ch, n],
                device_id=sibling,
                device_id_type=MESH,
            )

    for c in range(load_sem.shape[0]):
        load(c).start()
    @pl.loop(0, load_sem.shape[0])
    def _(c):
        load(c).wait()
        at = pl.ds(pl.multiple_of(c * strip, strip), strip)
        for p in range(0, aux_here, 16):
            turned[p : p + 16, at, :] = jnp.swapaxes(raw[at, p : p + 16, :], 0, 1)

    def forward(ch):
        for n in (2, 3, 0, 1):
            sent[ch, n].wait_recv()
            passed[ch, n].start()

    def arrived(ch):
        for n in range(len(STEPS)):
            passed[ch, n].wait_recv()

    def picked(ch, m):
        pieces = []
        for s in range(slots):
            piece = windows[ch][places[m][s]]
            pieces.append(jnp.where(s < counts[m], piece, jnp.zeros_like(piece)))
        return jnp.concatenate(pieces, axis=0)

    once = 1 + position // n_blk

    def contract(ch):
        @pl.loop(0, once)
        def _(_):
            for m in range(blocks):
                at = slice(m * width, (m + 1) * width)
                left = turned[:, at, :].reshape(aux_here * width, slots * width)
                got = jnp.dot(left, picked(ch, m), preferred_element_type=F32).astype(BF16)
                half[ch, :, at, :] = got.reshape(aux_here, width, CHUNK)

    def square(ch, part, parts):
        depth = aux_here // parts

        @pl.loop(part, part + once)
        def _(at):
            flat = [half[ch, at * depth + p] for p in range(depth)]
            flat = jnp.concatenate(flat, axis=1)
            got = lax.dot_general(flat, flat, (((1,), (1,)), ((), ())), preferred_element_type=F32)
            for q in range(rows // 128):
                gram[q] += got[:, 128 * q : 128 * q + 128]

    gram[...] = jnp.zeros_like(gram)
    for n in range(len(STEPS)):
        sent[0, n].wait_send()
        sent[1, n].start()
    forward(0)
    arrived(0)
    contract(0)
    square(0, 0, 2)
    forward(1)
    square(0, 1, 2)
    arrived(1)
    contract(1)
    square(1, 0, 1)

    low = lax.broadcasted_iota(jnp.int32, (width // 2, 128), 1) < width
    for j in range(blocks):
        for q in range(rows // 128):
            even = gram[q, pl.ds(j * width, width // 2, stride=2), :]
            odd = gram[q, pl.ds(j * width + 1, width // 2, stride=2), :]
            tiles[j * blocks + 2 * q] = jnp.where(low, even, pltpu.roll(odd, 64, 1))
            tiles[j * blocks + 2 * q + 1] = jnp.where(low, pltpu.roll(even, 64, 1), odd)
    far, home = 1 - y_lo, y_lo
    kept = total.shape[0]

    def lay_out(to_core, to_side):
        for t in range(kept):
            o = (to_side * 2 + to_core) * kept + t
            ready[to_core, to_side, t] = tiles[order[0, o]]

    def reduce_copy(src, dst, n, who):
        return pltpu.make_async_remote_copy(
            src_ref=src, dst_ref=dst, send_sem=red_send.at[n], recv_sem=red_recv.at[n],
            device_id=who, device_id_type=MESH,
        )

    away = reduce_copy(ready.at[1 - core, far], first_in.at[0], 0, sibling)
    here = reduce_copy(ready.at[1 - core, home], first_in.at[1], 1, sibling)
    cross = [
        reduce_copy(middle.at[half_at], second_in.at[half_at], 2 + n, across)
        for n, half_at in enumerate((pl.ds(0, kept // 2), pl.ds(kept // 2, kept // 2)))
    ]
    lay_out(1 - core, far)
    away.start()
    lay_out(core, far)
    away.wait_recv()
    for n in range(2):
        at = slice(n * (kept // 2), (n + 1) * (kept // 2))
        middle[at] = ready[core, far, at] + first_in[0, at]
        cross[n].start()
    lay_out(1 - core, home)
    here.start()
    lay_out(core, home)
    here.wait_recv()
    total[...] = ready[core, home] + first_in[1]
    for copy in [*(sent[1, n] for n in range(len(STEPS))), *passed.values(), away, here]:
        copy.wait_send()
    for n, copy in enumerate(cross):
        copy.wait_recv()
        at = slice(n * (kept // 2), (n + 1) * (kept // 2))
        total[at] = (total[at] + second_in[at]) * scale
        for s in range(total.shape[1]):
            out[at, 128 * s : 128 * s + 128] = total[at, s, :]
    for copy in cross:
        copy.wait_send()


def per_device(coeffs, fitting, screen, counts, tile_order):
    rows, orbitals = coeffs.shape
    _, aux_here, inner = fitting.shape
    blocks, _ = screen.shape
    chunks = orbitals // CHUNK
    near = len(STEPS)
    side = rows // blocks
    n_tiles = tile_order.shape[1]
    kept = n_tiles // lax.axis_size("aux")
    tile = (side * side // 128, 128)
    scale = 1.0 / (aux_here * lax.axis_size("aux") * orbitals) ** 0.5
    smem = pl.BlockSpec(memory_space=pltpu.SMEM)
    hbm = pl.BlockSpec(memory_space=pl.ANY)
    return pl.pallas_call(
        functools.partial(kernel, lax.axis_size("blk"), scale),
        out_shape=pltpu.VMEM((kept, side * side), F32),
        in_specs=[smem, smem, smem, hbm, hbm],
        out_specs=pl.BlockSpec(memory_space=pltpu.VMEM),
        scratch_shapes=[
            pltpu.VMEM((rows, aux_here, inner), BF16),
            pltpu.VMEM((aux_here, rows, inner), BF16),
            pltpu.VMEM(((near + 1) * blocks, side, CHUNK), BF16),
            pltpu.VMEM(((near + 1) * blocks, side, CHUNK), BF16),
            pltpu.VMEM((chunks, aux_here, rows, CHUNK), BF16),
            pltpu.VMEM((rows // 128, rows, 128), F32),
            pltpu.VMEM((n_tiles, *tile), F32),
            pltpu.VMEM((2, 2, kept, *tile), F32),
            pltpu.VMEM((2, kept, *tile), F32),
            pltpu.VMEM((kept, *tile), F32),
            pltpu.VMEM((kept, *tile), F32),
            pltpu.VMEM((kept, *tile), F32),
            pltpu.SemaphoreType.DMA((16,)),
            pltpu.SemaphoreType.DMA((chunks,)),
            pltpu.SemaphoreType.DMA((chunks, near)),
            pltpu.SemaphoreType.DMA((chunks, near)),
            pltpu.SemaphoreType.DMA((chunks, near)),
            pltpu.SemaphoreType.DMA((chunks, near)),
            pltpu.SemaphoreType.DMA((4,)),
            pltpu.SemaphoreType.DMA((4,)),
        ],
        compiler_params=pltpu.CompilerParams(
            collective_id=0, has_side_effects=True, vmem_limit_bytes=60 << 20
        ),
    )(screen, counts, tile_order, coeffs.reshape(blocks, side, orbitals), fitting)


def solution(mesh):
    placed = (P("blk", None), P("blk", "aux", None), P("blk", None), P("blk"), P("blk", None))
    with jax.sharding.use_abstract_mesh(mesh.abstract_mesh):
        return jax.shard_map(
            per_device, mesh=mesh, in_specs=placed, out_specs=P(("blk", "aux"), None), check_vma=False
        )
```
